32 devices in a mesh: sens: 2 (over x), sx: 4 (over z), sy: 4 (over y, core).
Axes of the slice: x: 2, y: 2, z: 4, core: 2. Of those that a mesh axis runs over, the one named last changes fastest.
Arguments:
- records: bfloat16 [4, 128, 128], P(None, 'sens'), may hold values from -6 to 6
- kernel: bfloat16 [128, 64, 32, 128], P('sens', 'sx', 'sy'), may hold values from -0.09375 to 0.09375
- diffusion: float32 [64, 32], P('sx', 'sy'), may hold values from 0.04 to 0.24
Outputs:
- predicted: float32 [4, 128, 128], P(None, ('sens', 'sx', 'sy'))
The draws below stay inside these ranges and needn't reach their ends.
All inputs are finite; a program needn't handle non-finite values.
Results may differ from the reference program's by a relative error of at most 0.0011.
Values may be sent and summed in bfloat16 or wider, within the bound.
A program may use at most 64 MiB of HBM per device.

```python
import math
import jax
import jax.numpy as jnp
from jax import lax

NT = 128
BATCH = 4
SWEEPS = 4
NS = 128
GX = 64
GY = 32


def draw_records(key, part):
    base = jnp.clip(jax.random.normal(key, (BATCH, NS, NT), jnp.float32), -6.0, 6.0)
    return base.astype(jnp.bfloat16)


def shard_levels(key, shape, split, smallest, largest):
    def one(axis_at, blocks):
        draws = jax.random.uniform(jax.random.fold_in(jax.random.fold_in(key, 6), axis_at), (blocks,), jnp.float32, smallest / len(split), largest / len(split))
        return jnp.repeat(jnp.exp(draws), shape[axis_at] // blocks).reshape((-1,) + (1,) * (len(shape) - axis_at - 1))

    gain = one(*split[0])
    for cut in split[1:]:
        gain = gain * one(*cut)
    return gain


def noise(key, extent, deviation, limit, split=(), held_as=jnp.bfloat16):
    drawn = deviation * jax.random.normal(key, extent, jnp.float32)
    if split:
        drawn = drawn * shard_levels(key, extent, split, -0.22, 0.18)
    return jnp.clip(drawn, -limit, limit).astype(held_as)


def setup_inputs(seed: int = 0) -> dict:
    arg_keys = jax.random.split(jax.random.key(seed), 4)
    records = draw_records(jax.random.fold_in(arg_keys[3], 71), 0)
    kernel = noise(arg_keys[1], (NS, GX, GY, NT), (1.6 / ((NS * GX * GY) ** 0.25 * NT ** 0.5)), 0.09375, ((0, 2), (1, 4), (2, 4)))
    diffusion = jnp.clip(jnp.exp(math.log(0.24) - 1.7917595 * jax.random.uniform(arg_keys[2], (GX, GY), jnp.float32) ** shard_levels(arg_keys[2], (GX, GY), ((0, 4), (1, 4)), -0.2, 0.2)), 0.04, 0.24)
    return dict(records=records, kernel=kernel, diffusion=diffusion)


def smooth(prior_field, diffusion):
    weights = diffusion[None, :, :, None]
    for repeat in range(SWEEPS):
        padded = jnp.pad(prior_field, ((0, 0), (1, 1), (1, 1), (0, 0)))
        beside_all = padded[:, 2:, 1:-1] + padded[:, :-2, 1:-1] + padded[:, 1:-1, 2:] + padded[:, 1:-1, :-2]
        prior_field = prior_field + weights * (beside_all - 4.0 * prior_field)
    return prior_field


def reference(records, kernel, diffusion):
    groups = NS // 64
    kernel_blocks = kernel.reshape(groups, 64, GX * GY, NT)
    data_blocks = records.reshape(BATCH, groups, 64, NT).transpose(1, 0, 2, 3)

    def adjoint_step(running, couple):
        kernel_block, data_block = couple
        portion = lax.conv_general_dilated(
            data_block.astype(jnp.float32), kernel_block.astype(jnp.float32), (1,), [(0, NT - 1)],
            dimension_numbers=("NCH", "IOH", "NCH"), precision=lax.Precision.HIGHEST)
        return running + portion, None

    adjoint_field, _ = lax.scan(adjoint_step, jnp.zeros((BATCH, GX * GY, NT), jnp.float32),
                                (kernel_blocks, data_blocks))
    prior_field = smooth(adjoint_field.reshape(BATCH, GX, GY, NT), diffusion)
    smoothed = prior_field.astype(jnp.bfloat16).astype(jnp.float32)
    flipped = smoothed.reshape(BATCH, GX * GY, NT)[:, :, ::-1]

    def forward_block(kernel_block):
        backward = lax.conv_general_dilated(
            flipped, kernel_block.astype(jnp.float32), (1,), [(0, NT - 1)],
            dimension_numbers=("NCH", "OIH", "NCH"), precision=lax.Precision.HIGHEST)
        return backward[:, :, ::-1]

    results = lax.map(forward_block, kernel_blocks)
    return results.transpose(1, 0, 2, 3).reshape(BATCH, NS, NT)
```

```python
import functools

import jax
import jax.numpy as jnp
from jax import lax
from jax.experimental import pallas as pl
from jax.experimental.pallas import tpu as pltpu
from jax.sharding import PartitionSpec as P

SWEEPS = 4
MESH = pl.DeviceIdType.MESH
F32 = jnp.float32
BF16 = jnp.bfloat16
DIRECTIONS = ((-1, 0), (1, 0), (0, -1), (0, 1), (-1, -1), (-1, 1), (1, -1), (1, 1))
STEP = 8
PACK = 16
NT = (((1,), (1,)), ((), ()))


def opposite(d):
    dx, dy = DIRECTIONS[d]
    return DIRECTIONS.index((-dx, -dy))


def iota(shape, axis):
    return lax.broadcasted_iota(jnp.int32, shape, axis)


class Grid:
    def __init__(self, sizes, cells_x, cells_y):
        self.nx, self.ny = sizes
        self.cx, self.cy, self.m = cells_x, cells_y, SWEEPS
        self.points = cells_x * cells_y
        self.counts = [self.m * self.cy if dy == 0 else self.cx * self.m if dx == 0 else self.m * self.m
                       for dx, dy in DIRECTIONS]
        self.offsets = [sum(self.counts[:d]) for d in range(len(DIRECTIONS))]
        self.halo = sum(self.counts)
        self.mx, self.my = lax.axis_index("sx"), lax.axis_index("sy")

    def exists(self, d):
        dx, dy = DIRECTIONS[d]
        ok = jnp.bool_(True)
        if dx:
            ok = ok & (self.mx + dx >= 0) & (self.mx + dx < self.nx)
        if dy:
            ok = ok & (self.my + dy >= 0) & (self.my + dy < self.ny)
        return ok

    def each(self, act):
        for d in range(len(DIRECTIONS)):
            @pl.when(self.exists(d))
            def _():
                act(d)

    def neighbour(self, d):
        dx, dy = DIRECTIONS[d]
        return {"sx": self.mx + dx, "sy": self.my + dy}

    def neighbours(self):
        wide_x = 1 + (self.mx > 0).astype(jnp.int32) + (self.mx < self.nx - 1).astype(jnp.int32)
        wide_y = 1 + (self.my > 0).astype(jnp.int32) + (self.my < self.ny - 1).astype(jnp.int32)
        return wide_x * wide_y - 1

    def selection(self):
        rows = []
        for (dx, dy), count in zip(DIRECTIONS, self.counts):
            r, p = iota((count, self.points), 0), iota((count, self.points), 1)
            x0 = self.cx - self.m if dx > 0 else 0
            if dy == 0:
                source = x0 * self.cy + r
            else:
                y0 = self.cy - self.m if dy > 0 else 0
                source = (x0 + r // self.m) * self.cy + y0 + r % self.m
            rows.append((p == source).astype(F32))
        return jnp.concatenate(rows, axis=0).astype(BF16)

    def place(self, wide_x):
        if wide_x < self.m:
            return -1, wide_x
        if wide_x < self.m + self.cx:
            return 0, wide_x - self.m
        return 1, wide_x - self.m - self.cx

    def index(self, wide_x):
        at, local = self.place(wide_x)
        sub = iota((self.cy, 128), 0)

        def base(dy):
            return self.points + self.offsets[DIRECTIONS.index((at, dy))]

        own = (local * self.cy if at == 0 else base(0) + local * self.cy) + sub
        right = base(1) + local * self.m + sub
        left = base(-1) + local * self.m + sub - self.m
        return own, jnp.where(sub < self.m, right, left)


def row_sums(terms):
    row = iota(terms[0].shape, 0)

    def merge(a, b, take, shift):
        return jnp.where(take, a, b) + pltpu.roll(jnp.where(take, b, a), 8 - shift, 0)

    sides = []
    for o in range(2):
        pair = [merge(terms[o + 2 * e], terms[o + 2 * e + 4], ((row - o - 2 * e) & 7) < 4, 4) for e in range(2)]
        sides.append(merge(pair[0], pair[1], ((row - o) & 3) < 2, 2))
    return merge(sides[0], sides[1], (row & 1) == 0, 1)


def kernel(sizes, vectors, sensors, cells_x, cells_y, window,
           records_hbm, rates_hbm, kernel_hbm, out_ref,
           rec, recf, rates, tile_d, got_d, wide_d, kbuf, kshift, hankel, acc,
           part, got, select, hi, lo, halo_out, halo_in, map_hi, map_lo, smooth_t, pred, pred_got,
           i_sem, k_sem, s_send, s_recv, d_send, d_recv, h_send, h_recv, p_send, p_recv, ready):
    n_s, n_x, n_y = sizes
    points = cells_x * cells_y
    half = window // 2
    per = window // half
    pairs = vectors // per
    chunks = 2 * pairs
    n_q = n_x * n_y
    group = sensors // n_q
    steps = sensors // STEP
    me_s, me_x, me_y = lax.axis_index("sens"), lax.axis_index("sx"), lax.axis_index("sy")
    me_q = me_x * n_y + me_y
    grid = Grid((n_x, n_y), cells_x, cells_y)

    r_copy = pltpu.make_async_copy(records_hbm, rec, i_sem.at[0])
    d_copy = pltpu.make_async_copy(rates_hbm, rates, i_sem.at[1])

    def k_copy(i):
        return pltpu.make_async_copy(
            kernel_hbm.at[pl.ds(i * STEP, STEP)], kbuf.at[pl.ds(i * STEP, STEP)], k_sem.at[i])

    r_copy.start()
    d_copy.start()
    for i in range(steps):
        k_copy(i).start()

    halo_in[...] = jnp.zeros_like(halo_in)
    got_d[...] = jnp.zeros_like(got_d)

    barrier = pltpu.get_barrier_semaphore()
    for k in range(1, n_s):
        pl.semaphore_signal(barrier, inc=1, device_id={"sens": lax.rem(me_s + k, n_s)}, device_id_type=MESH)
    grid.each(lambda d: pl.semaphore_signal(barrier, inc=1, device_id=grid.neighbour(d), device_id_type=MESH))

    select[...] = grid.selection()
    lanes, rows = iota((PACK, window), 1), iota((PACK, window), 0)
    keep = [(lanes < window - half + 1 + PACK * j + rows).astype(F32).astype(BF16) for j in range(half // PACK)]
    late = (iota((points, window), 1) >= half).astype(F32).astype(BF16)

    r_copy.wait()
    for v in range(vectors):
        recf[v] = rec[v].astype(F32)

    def build(i, _):
        for v in range(vectors):
            block = recf[v, pl.ds(pl.multiple_of(i * STEP, STEP), STEP)]
            for s in range(STEP):
                line = jnp.broadcast_to(block[s:s + 1], (PACK, window))
                seed = pltpu.roll(line, window - half + 1, 1, stride=1, stride_axis=0).astype(BF16)
                for j in range(half // PACK):
                    turned = seed if j == 0 else pltpu.roll(seed, PACK * j, 1)
                    hankel[i, pl.ds(v * half + j * PACK, PACK), pl.ds(s * window, window)] = turned * keep[j]
        return 0

    lax.fori_loop(0, steps, build, 0)

    acc[...] = jnp.zeros_like(acc)

    def adjoint(i, _):
        k_copy(i).wait()
        plain, moved = [], []
        for s in range(STEP):
            block = kbuf[i * STEP + s]
            shifted = pltpu.roll(block, half, 1) * late
            kshift[i * STEP + s] = shifted
            plain.append(block)
            moved.append(shifted)
        lhs = jnp.concatenate([jnp.concatenate(plain, axis=1), jnp.concatenate(moved, axis=1)], axis=0)
        acc[...] += lax.dot_general(lhs, hankel[i], NT, preferred_element_type=F32)
        return 0

    lax.fori_loop(0, steps, adjoint, 0)

    def at(c):
        return pl.ds((c % 2) * points, points), pl.ds((c // 2) * window, window)

    def s_copy(hop, c):
        return pltpu.make_async_remote_copy(
            src_ref=part.at[c], dst_ref=got.at[hop - 1, c],
            send_sem=s_send.at[hop - 1, c], recv_sem=s_recv.at[hop - 1, c],
            device_id={"sens": lax.rem(me_s + hop, n_s)}, device_id_type=MESH)

    def e_copy(d):
        return pltpu.make_async_remote_copy(
            src_ref=tile_d, dst_ref=got_d.at[opposite(d)], send_sem=d_send.at[d], recv_sem=d_recv.at[opposite(d)],
            device_id=grid.neighbour(d), device_id_type=MESH)

    def h_copy(c, d):
        o = opposite(d)
        return pltpu.make_async_remote_copy(
            src_ref=halo_out.at[c, pl.ds(grid.offsets[d], grid.counts[d])],
            dst_ref=halo_in.at[c, pl.ds(grid.offsets[o], grid.counts[o])],
            send_sem=h_send.at[c, d], recv_sem=h_recv.at[c, o],
            device_id=grid.neighbour(d), device_id_type=MESH)

    d_copy.wait()
    tile_d[...] = jnp.zeros_like(tile_d)
    tile_d[:, :cells_x] = rates[...]
    for c in range(chunks):
        part[c] = acc[at(c)].astype(BF16)

    pl.semaphore_wait(barrier, n_s - 1 + grid.neighbours())
    for c in range(chunks):
        for hop in range(1, n_s):
            s_copy(hop, c).start()
    grid.each(lambda d: e_copy(d).start())
    grid.each(lambda d: e_copy(opposite(d)).wait_recv())

    sub = iota((cells_y, window), 0)
    m = grid.m
    wide_x = cells_x + 2 * m
    units = []
    for x in range(wide_x):
        where_x, local = grid.place(x)
        column = local + (cells_x - m if where_x < 0 else 0)

        def rate(dy):
            d = (where_x, dy)
            block = tile_d[...] if d == (0, 0) else got_d[DIRECTIONS.index(d)]
            return jnp.broadcast_to(block[:, column:column + 1], (cells_y, window))

        wide_d[x, pl.ds(0, cells_y)] = rate(0)
        wide_d[x, pl.ds(cells_y, cells_y)] = jnp.where(sub < m, rate(1), rate(-1))

    def sweep_map(t, _):
        lane = iota((cells_y, window), 1) + t * window
        units = []
        for x in range(wide_x):
            own, beside = grid.index(x)
            units.append(jnp.concatenate([(lane == own).astype(F32), (lane == beside).astype(F32)], axis=0))
        now = jnp.stack(units, axis=0)
        for repeat in range(SWEEPS):
            interior = now[1:-1]
            beside = now[2:] + now[:-2] + pltpu.roll(interior, 2 * cells_y - 1, 1) + pltpu.roll(interior, 1, 1)
            rate = wide_d[pl.ds(repeat + 1, cells_x + 2 * (m - repeat - 1))]
            now = interior + rate * (beside - 4.0 * interior)
        done = now[:, :cells_y].reshape(points, window)
        top = done.astype(BF16)
        map_hi[t] = top
        map_lo[t] = (done - top.astype(F32)).astype(BF16)
        return 0

    lax.fori_loop(0, (points + grid.halo) // window, sweep_map, 0)

    for c in range(chunks):
        total = acc[at(c)]
        for hop in range(1, n_s):
            s_copy(hop, c).wait_recv()
            total = total + got[hop - 1, c].astype(F32)
        top = total.astype(BF16)
        hi[c] = top
        lo[c] = (total - top.astype(F32)).astype(BF16)
        halo_out[c] = jnp.dot(select[...], top, preferred_element_type=F32).astype(BF16)
        grid.each(lambda d: h_copy(c, d).start())

    turn_r, turn_c = iota((window, window), 0), iota((window, window), 1)
    turn = ((turn_r // half == turn_c // half) & (turn_r % half + turn_c % half == half - 1)).astype(F32).astype(BF16)
    tiles = (points + grid.halo) // window
    first = jnp.concatenate([map_hi[0], map_hi[0]] + [map_hi[t] for t in range(1, tiles)], axis=1)
    second = jnp.concatenate([map_lo[t] for t in range(tiles)], axis=1)
    for c in range(chunks):
        grid.each(lambda d: h_copy(c, opposite(d)).wait_recv())
        done = jnp.dot(first, jnp.concatenate([hi[c], lo[c], halo_in[c]], axis=0), preferred_element_type=F32)
        done = done + jnp.dot(second, jnp.concatenate([hi[c], halo_in[c]], axis=0), preferred_element_type=F32)
        smooth_t[pl.ds((c // 2) * window, window), pl.ds((c % 2) * points, points)] = lax.dot_general(
            turn, done.astype(BF16), NT, preferred_element_type=F32).astype(BF16)

    reach = max(n_x, n_y) - 1
    for r in range(max(reach - 3, 0)):
        grid.each(lambda d: pl.semaphore_signal(ready.at[r], inc=1, device_id=grid.neighbour(d), device_id_type=MESH))
        pl.semaphore_wait(ready.at[r], grid.neighbours())

    lanes8, rows8 = iota((8, window), 1), iota((8, window), 0)
    bits = n_q.bit_length() - 1

    def partner(k):
        if n_q != 1 << bits:
            return lax.rem(me_q + k, n_q)
        total = 0
        for b in range(bits):
            one, two = lax.rem(me_q // (1 << b), 2), lax.rem(k // (1 << b), 2)
            total = total + (one + two - 2 * one * two) * (1 << b)
        return total

    def p_copy(k):
        q = partner(k)
        return pltpu.make_async_remote_copy(
            src_ref=pred.at[q], dst_ref=pred_got.at[k - 1],
            send_sem=p_send.at[k - 1], recv_sem=p_recv.at[k - 1],
            device_id={"sx": q // n_y, "sy": lax.rem(q, n_y)}, device_id_type=MESH)

    def diagonal(tile):
        terms = [tile[8 * j:8 * j + 8] for j in range(half // 8)]
        by = 8
        while len(terms) > 1:
            terms = [a + jnp.where(lanes8 >= by, pltpu.roll(b, by, 1), 0.0) for a, b in zip(terms[::2], terms[1::2])]
            by *= 2
        return jnp.where(lanes8 >= rows8, pltpu.roll(terms[0], 0, 1, stride=1, stride_axis=0), 0.0)

    unroll = max(u for u in range(1, n_q + 1) if n_q % u == 0 and u * group <= 8)

    def forward(i, _):
        for u in range(unroll):
            q = partner(n_q - 1 - (i * unroll + u))
            rhs = jnp.concatenate([
                jnp.concatenate([buf[q * group + s] for s in range(group)], axis=1) for buf in (kbuf, kshift)], axis=0)
            res = jnp.dot(smooth_t[...], rhs, preferred_element_type=F32)
            runs = [diagonal(res[v * half:(v + 1) * half, s * window:(s + 1) * window])
                    for v in range(vectors) for s in range(group)]
            count = len(runs)
            runs += [jnp.zeros_like(runs[0])] * (-count % 8)
            pred[q] = jnp.concatenate([row_sums(runs[j:j + 8]) for j in range(0, len(runs), 8)], axis=0)[:count]
        for u in range(unroll):
            k = n_q - 1 - (i * unroll + u)

            @pl.when(k > 0)
            def _():
                p_copy(k).start()
        return 0

    lax.fori_loop(0, n_q // unroll, forward, 0)

    def finish(k, total):
        p_copy(k).wait_recv()
        return total + pred_got[k - 1]

    total = lax.fori_loop(1, n_q, finish, pred[me_q])
    for v in range(vectors):
        out_ref[v] = total[v * group:(v + 1) * group]

    def drain(k, _):
        p_copy(k).wait_send()
        return 0

    lax.fori_loop(1, n_q, drain, 0)
    grid.each(lambda d: e_copy(d).wait_send())
    for c in range(chunks):
        for hop in range(1, n_s):
            s_copy(hop, c).wait_send()
        grid.each(lambda d: h_copy(c, d).wait_send())


def per_device(sizes, records, kernel_block, diffusion):
    vectors, sensors, window = records.shape
    cells_x, cells_y = diffusion.shape
    points = cells_x * cells_y
    n_s, n_x, n_y = sizes
    n_q = n_x * n_y
    group = sensors // n_q
    half = window // 2
    chunks = vectors * half // window * 2
    steps = sensors // STEP
    halo = (cells_x + 2 * SWEEPS) * (cells_y + 2 * SWEEPS) - points
    tiles = (points + halo) // window
    around = len(DIRECTIONS)
    kernel_rows = kernel_block.reshape(sensors, points, window)
    rates = diffusion.T
    hops = max(n_s - 1, 1)
    dma = pltpu.SemaphoreType.DMA
    vmem = pltpu.VMEM
    return pl.pallas_call(
        functools.partial(kernel, sizes, vectors, sensors, cells_x, cells_y, window),
        out_shape=vmem((vectors, group, window), F32),
        in_specs=[pl.BlockSpec(memory_space=pl.ANY)] * 3,
        out_specs=pl.BlockSpec(memory_space=vmem),
        scratch_shapes=[
            vmem((vectors, sensors, window), BF16),
            vmem((vectors, sensors, window), F32),
            vmem((cells_y, cells_x), F32),
            vmem((cells_y, window), F32),
            vmem((around, cells_y, window), F32),
            vmem((cells_x + 2 * SWEEPS, 2 * cells_y, window), F32),
            vmem((sensors, points, window), BF16),
            vmem((sensors, points, window), BF16),
            vmem((steps, vectors * half, STEP * window), BF16),
            vmem((2 * points, vectors * half), F32),
            vmem((chunks, points, window), BF16),
            vmem((hops, chunks, points, window), BF16),
            vmem((halo, points), BF16),
            vmem((chunks, points, window), BF16),
            vmem((chunks, points, window), BF16),
            vmem((chunks, halo, window), BF16),
            vmem((chunks, halo, window), BF16),
            vmem((tiles, points, window), BF16),
            vmem((tiles, points, window), BF16),
            vmem((vectors * half, 2 * points), BF16),
            vmem((n_q, vectors * group, window), F32),
            vmem((max(n_q - 1, 1), vectors * group, window), F32),
            dma((2,)),
            dma((steps,)),
            *[dma((hops, chunks))] * 2,
            *[dma((around,))] * 2,
            *[dma((chunks, around))] * 2,
            *[dma((max(n_q - 1, 1),))] * 2,
            pltpu.SemaphoreType.REGULAR((max(max(n_x, n_y) - 4, 1),)),
        ],
        compiler_params=pltpu.CompilerParams(collective_id=0, has_side_effects=True),
    )(records, rates, kernel_rows)


def solution(mesh):
    sizes = tuple(mesh.shape[a] for a in ("sens", "sx", "sy"))
    return jax.shard_map(
        functools.partial(per_device, sizes),
        mesh=mesh,
        in_specs=(P(None, "sens", None), P("sens", "sx", "sy", None), P("sx", "sy")),
        out_specs=P(None, ("sens", "sx", "sy"), None),
        check_vma=False,
    )
```

```python
import functools

import jax
import jax.numpy as jnp
from jax import lax
from jax.experimental import pallas as pl
from jax.experimental.pallas import tpu as pltpu
from jax.sharding import PartitionSpec as P

SWEEPS = 4
MESH = pl.DeviceIdType.MESH
F32 = jnp.float32
BF16 = jnp.bfloat16
DIRECTIONS = ((-1, 0), (1, 0), (0, -1), (0, 1), (-1, -1), (-1, 1), (1, -1), (1, 1))
STEP = 16
PACK = 16
GROUP = 2
WIDE = 2
BATCH = 4
NT = (((1,), (1,)), ((), ()))


def opposite(d):
    dx, dy = DIRECTIONS[d]
    return DIRECTIONS.index((-dx, -dy))


def iota(shape, axis):
    return lax.broadcasted_iota(jnp.int32, shape, axis)


class Grid:
    def __init__(self, sizes, cells_x, cells_y):
        self.nx, self.ny = sizes
        self.cx, self.cy, self.m = cells_x, cells_y, SWEEPS
        self.points = cells_x * cells_y
        self.counts = [self.m * self.cy if dy == 0 else self.cx * self.m if dx == 0 else self.m * self.m
                       for dx, dy in DIRECTIONS]
        self.offsets = [sum(self.counts[:d]) for d in range(len(DIRECTIONS))]
        self.halo = sum(self.counts)
        self.mx, self.my = lax.axis_index("sx"), lax.axis_index("sy")

    def exists(self, d):
        dx, dy = DIRECTIONS[d]
        ok = jnp.bool_(True)
        if dx:
            ok = ok & (self.mx + dx >= 0) & (self.mx + dx < self.nx)
        if dy:
            ok = ok & (self.my + dy >= 0) & (self.my + dy < self.ny)
        return ok

    def each(self, act):
        for d in range(len(DIRECTIONS)):
            @pl.when(self.exists(d))
            def _():
                act(d)

    def neighbour(self, d):
        dx, dy = DIRECTIONS[d]
        return {"sx": self.mx + dx, "sy": self.my + dy}

    def neighbours(self):
        wide_x = 1 + (self.mx > 0).astype(jnp.int32) + (self.mx < self.nx - 1).astype(jnp.int32)
        wide_y = 1 + (self.my > 0).astype(jnp.int32) + (self.my < self.ny - 1).astype(jnp.int32)
        return wide_x * wide_y - 1

    def selection(self):
        rows = []
        for (dx, dy), count in zip(DIRECTIONS, self.counts):
            r, p = iota((count, self.points), 0), iota((count, self.points), 1)
            x0 = self.cx - self.m if dx > 0 else 0
            if dy == 0:
                source = x0 * self.cy + r
            else:
                y0 = self.cy - self.m if dy > 0 else 0
                source = (x0 + r // self.m) * self.cy + y0 + r % self.m
            rows.append((p == source).astype(F32))
        return jnp.concatenate(rows, axis=0).astype(BF16)

    def place(self, wide_x):
        if wide_x < self.m:
            return -1, wide_x
        if wide_x < self.m + self.cx:
            return 0, wide_x - self.m
        return 1, wide_x - self.m - self.cx

    def index(self, wide_x):
        at, local = self.place(wide_x)
        sub = iota((self.cy, 128), 0)

        def base(dy):
            return self.points + self.offsets[DIRECTIONS.index((at, dy))]

        own = (local * self.cy if at == 0 else base(0) + local * self.cy) + sub
        right = base(1) + local * self.m + sub
        left = base(-1) + local * self.m + sub - self.m
        return own, jnp.where(sub < self.m, right, left)


def row_sums(terms):
    row = iota(terms[0].shape, 0)

    def merge(a, b, take, shift):
        return jnp.where(take, a, b) + pltpu.roll(jnp.where(take, b, a), 8 - shift, 0)

    sides = []
    for o in range(2):
        pair = [merge(terms[o + 2 * e], terms[o + 2 * e + 4], ((row - o - 2 * e) & 7) < 4, 4) for e in range(2)]
        sides.append(merge(pair[0], pair[1], ((row - o) & 3) < 2, 2))
    return merge(sides[0], sides[1], (row & 1) == 0, 1)


def kernel(sizes, vectors, sensors, cells_x, cells_y, window,
           records_hbm, rates_hbm, kernel_hbm, out_ref,
           rec, recf, rates, tile_d, got_d, wide_d, kbuf, kshift, acc,
           part, got, select, hi, lo, halo_out, halo_in, map_hi, map_lo, smooth_t, pred, pred_got,
           i_sem, k_sem, s_send, s_recv, d_send, d_recv, h_send, h_recv, p_send, p_recv, ready):
    n_s, n_x, n_y = sizes
    points = cells_x * cells_y
    half = window // 2
    pairs = vectors // 2
    n_q = n_x * n_y
    group = sensors // n_q
    steps = sensors // STEP
    me_s, me_x, me_y = lax.axis_index("sens"), lax.axis_index("sx"), lax.axis_index("sy")
    grid = Grid((n_x, n_y), cells_x, cells_y)

    r_copy = pltpu.make_async_copy(records_hbm, rec, i_sem.at[0])
    d_copy = pltpu.make_async_copy(rates_hbm, rates, i_sem.at[1])

    def k_copy(i):
        return pltpu.make_async_copy(
            kernel_hbm.at[pl.ds(i * STEP, STEP)], kbuf.at[pl.ds(i * STEP, STEP)], k_sem.at[i])

    r_copy.start()
    d_copy.start()
    for i in range(steps):
        k_copy(i).start()

    barrier = pltpu.get_barrier_semaphore()
    got_d[...] = jnp.zeros_like(got_d)
    halo_in[...] = jnp.zeros_like(halo_in)
    for k in range(1, n_s):
        pl.semaphore_signal(barrier, inc=1, device_id={"sens": lax.rem(me_s + k, n_s)}, device_id_type=MESH)
    grid.each(lambda d: pl.semaphore_signal(barrier, inc=1, device_id=grid.neighbour(d), device_id_type=MESH))

    lanes, rows = iota((PACK, window), 1), iota((PACK, window), 0)
    keep = [(lanes < window - half + 1 + PACK * j + rows).astype(F32).astype(BF16) for j in range(half // PACK)]
    late = (iota((points, window), 1) >= half).astype(F32).astype(BF16)

    r_copy.wait()
    for v in range(vectors):
        recf[v] = rec[v].astype(F32)

    def hankel(v, block, s):
        line = jnp.broadcast_to(block[s:s + 1], (PACK, window))
        seed = pltpu.roll(line, window - half + 1, 1, stride=1, stride_axis=0).astype(BF16)
        return jnp.concatenate(
            [(seed if j == 0 else pltpu.roll(seed, PACK * j, 1)) * keep[j] for j in range(half // PACK)], axis=0)

    def lagged(s):
        block = kbuf[s]
        moved = pltpu.roll(block, half, 1) * late
        kshift[0, s] = moved
        return jnp.concatenate([block, moved], axis=0)

    acc[...] = jnp.zeros_like(acc)

    def adjoint(i, _):
        k_copy(i).wait()
        blocks = [recf[v, pl.ds(pl.multiple_of(i * STEP, STEP), STEP)] for v in range(vectors)]
        for g in range(0, STEP, GROUP):
            rhs = jnp.concatenate([
                jnp.concatenate([hankel(v, blocks[v], s) for v in range(vectors)], axis=0) for s in range(g, g + GROUP)], axis=1)
            lhs = jnp.concatenate([lagged(i * STEP + s) for s in range(g, g + GROUP)], axis=1)
            acc[...] += lax.dot_general(lhs, rhs, NT, preferred_element_type=F32)
        return 0

    lax.fori_loop(0, steps, adjoint, 0)

    def s_copy(hop, c):
        return pltpu.make_async_remote_copy(
            src_ref=part.at[c], dst_ref=got.at[hop - 1, c],
            send_sem=s_send.at[hop - 1, c], recv_sem=s_recv.at[hop - 1, c],
            device_id={"sens": lax.rem(me_s + hop, n_s)}, device_id_type=MESH)

    def e_copy(d):
        return pltpu.make_async_remote_copy(
            src_ref=tile_d, dst_ref=got_d.at[opposite(d)], send_sem=d_send.at[d], recv_sem=d_recv.at[opposite(d)],
            device_id=grid.neighbour(d), device_id_type=MESH)

    def h_copy(c, d):
        o = opposite(d)
        return pltpu.make_async_remote_copy(
            src_ref=halo_out.at[c, :, pl.ds(grid.offsets[d], grid.counts[d])],
            dst_ref=halo_in.at[c, :, pl.ds(grid.offsets[o], grid.counts[o])],
            send_sem=h_send.at[c, d], recv_sem=h_recv.at[c, o],
            device_id=grid.neighbour(d), device_id_type=MESH)

    d_copy.wait()
    tile_d[...] = jnp.zeros_like(tile_d)
    tile_d[:, :cells_x] = rates[...]
    for c in range(pairs):
        for h in range(2):
            part[c, h] = acc[pl.ds(h * points, points), pl.ds(c * window, window)].astype(BF16)

    pl.semaphore_wait(barrier, n_s - 1 + grid.neighbours())
    for c in range(pairs):
        for hop in range(1, n_s):
            s_copy(hop, c).start()
    grid.each(lambda d: e_copy(d).start())
    select[...] = grid.selection()

    quarter = half // 2
    later = [(iota((points, window), 1) >= by).astype(F32).astype(BF16) for by in (quarter, half + quarter)]

    def shifts(i, _):
        for u in range(4):
            block = kbuf[4 * i + u]
            for j, by in enumerate((quarter, half + quarter)):
                kshift[j + 1, 4 * i + u] = pltpu.roll(block, by, 1) * later[j]
        return 0

    lax.fori_loop(0, sensors // 4, shifts, 0)

    def gather(c):
        for hop in range(1, n_s):
            s_copy(hop, c).wait_recv()
        for h in range(2):
            total = acc[pl.ds(h * points, points), pl.ds(c * window, window)]
            for hop in range(1, n_s):
                total = total + got[hop - 1, c, h].astype(F32)
            top = total.astype(BF16)
            hi[c, h] = top
            lo[c, h] = (total - top.astype(F32)).astype(BF16)
        beside = jnp.dot(select[...], jnp.concatenate([hi[c, 0], hi[c, 1]], axis=1), preferred_element_type=F32)
        for h in range(2):
            halo_out[c, h] = beside[:, h * window:(h + 1) * window].astype(BF16)
        grid.each(lambda d: h_copy(c, d).start())

    for c in range(pairs):
        gather(c)

    reach = max(n_x, n_y) - 1

    def call(r):
        grid.each(lambda d: pl.semaphore_signal(ready.at[r], inc=1, device_id=grid.neighbour(d), device_id_type=MESH))

    def answer(r):
        pl.semaphore_wait(ready.at[r], grid.neighbours())

    grid.each(lambda d: e_copy(opposite(d)).wait_recv())
    if reach > 2:
        call(0)

    sub = iota((cells_y, window), 0)
    m = grid.m
    wide_x = cells_x + 2 * m
    for x in range(wide_x):
        where_x, local = grid.place(x)
        column = local + (cells_x - m if where_x < 0 else 0)

        def rate(dy):
            d = (where_x, dy)
            block = tile_d[...] if d == (0, 0) else got_d[DIRECTIONS.index(d)]
            return jnp.broadcast_to(block[:, column:column + 1], (cells_y, window))

        wide_d[x, pl.ds(0, cells_y)] = rate(0)
        wide_d[x, pl.ds(cells_y, cells_y)] = jnp.where(sub < m, rate(1), rate(-1))

    def sweep_map(t, _):
        lane = iota((cells_y, window), 1) + t * window
        units = []
        for x in range(wide_x):
            own, beside = grid.index(x)
            units.append(jnp.concatenate([(lane == own).astype(F32), (lane == beside).astype(F32)], axis=0))
        now = jnp.stack(units, axis=0)
        for repeat in range(SWEEPS):
            interior = now[1:-1]
            beside = now[2:] + now[:-2] + pltpu.roll(interior, 2 * cells_y - 1, 1) + pltpu.roll(interior, 1, 1)
            rate = wide_d[pl.ds(repeat + 1, cells_x + 2 * (m - repeat - 1))]
            now = interior + rate * (beside - 4.0 * interior)
        done = now[:, :cells_y].reshape(points, window)
        top = done.astype(BF16)
        map_hi[t] = top
        map_lo[t] = (done - top.astype(F32)).astype(BF16)
        return 0

    tiles = (points + grid.halo) // window
    lax.fori_loop(0, tiles, sweep_map, 0)

    turn_r, turn_c = iota((window, window), 0), iota((window, window), 1)
    turn = ((turn_r // half == turn_c // half) & (turn_r % half + turn_c % half == half - 1)).astype(F32).astype(BF16)

    def smooth(c):
        grid.each(lambda d: h_copy(c, opposite(d)).wait_recv())
        first = jnp.concatenate([map_hi[0], map_hi[0]] + [map_hi[t] for t in range(1, tiles)], axis=1)
        second = jnp.concatenate([map_lo[t] for t in range(tiles)], axis=1)
        tall = jnp.concatenate([
            jnp.concatenate([hi[c, h], lo[c, h], halo_in[c, h]], axis=0) for h in range(2)], axis=1)
        short = jnp.concatenate([jnp.concatenate([hi[c, h], halo_in[c, h]], axis=0) for h in range(2)], axis=1)
        done = jnp.dot(first, tall, preferred_element_type=F32) + jnp.dot(second, short, preferred_element_type=F32)
        for h in range(2):
            turned = lax.dot_general(
                turn, done[:, h * window:(h + 1) * window].astype(BF16), NT, preferred_element_type=F32).astype(BF16)
            for v in range(2):
                for e in range(2):
                    smooth_t[2 * h + e, pl.ds((2 * c + v) * quarter, quarter)] = turned[
                        v * half + e * quarter:v * half + (e + 1) * quarter]

    lanes8, rows8 = iota((8, window), 1), iota((8, window), 0)

    def partner(me, k, n):
        bits = n.bit_length() - 1
        if n != 1 << bits:
            return lax.rem(me + k, n)
        total = 0
        for b in range(bits):
            one = lax.rem(me // (1 << b), 2)
            two = (k >> b) & 1 if isinstance(k, int) else lax.rem(k // (1 << b), 2)
            total = total + (one + two - 2 * one * two) * (1 << b)
        return total

    def p_copy(kx, ky):
        x, y = partner(me_x, kx, n_x), partner(me_y, ky, n_y)
        k = kx * n_y + ky
        return pltpu.make_async_remote_copy(
            src_ref=pred.at[x * n_y + y], dst_ref=pred_got.at[k - 1],
            send_sem=p_send.at[k - 1], recv_sem=p_recv.at[k - 1],
            device_id={"sx": x, "sy": y}, device_id_type=MESH)

    def diagonal(tile):
        terms = [tile[8 * j:8 * j + 8] for j in range(quarter // 8)]
        by = 8
        while len(terms) > 1:
            terms = [a + jnp.where(lanes8 >= by, pltpu.roll(b, by, 1), 0.0) for a, b in zip(terms[::2], terms[1::2])]
            by *= 2
        return jnp.where(lanes8 >= rows8, pltpu.roll(terms[0], 0, 1, stride=1, stride_axis=0), 0.0)

    for c in range(pairs):
        smooth(c)
    if reach > 2:
        answer(0)
        for r in range(1, reach - 2):
            call(r)
            answer(r)

    lhs = jnp.concatenate([smooth_t[h] for h in range(4)], axis=1)
    for k in reversed(range(n_q)):
        q = partner(me_x, k // n_y, n_x) * n_y + partner(me_y, k % n_y, n_y)
        runs = [None] * (vectors * group)
        for g in range(0, group, WIDE):
            some = range(g, min(g + WIDE, group))
            rhs = jnp.concatenate([
                jnp.concatenate([buf[q * group + s] for s in some], axis=1)
                for buf in (kbuf, kshift.at[1], kshift.at[0], kshift.at[2])], axis=0)
            res = jnp.dot(lhs, rhs, preferred_element_type=F32)
            for v in range(vectors):
                for s in some:
                    runs[v * group + s] = diagonal(
                        res[v * quarter:(v + 1) * quarter, (s - g) * window:(s - g + 1) * window])
        count = len(runs)
        runs += [jnp.zeros_like(runs[0])] * (-count % 8)
        pred[q] = jnp.concatenate([row_sums(runs[j:j + 8]) for j in range(0, len(runs), 8)], axis=0)[:count]
        if k % BATCH == 0:
            for j in reversed(range(max(k, 1), min(k + BATCH, n_q))):
                p_copy(j // n_y, j % n_y).start()

    def finish(k, total):
        p_copy(k // n_y, lax.rem(k, n_y)).wait_recv()
        return total + pred_got[k - 1]

    total = lax.fori_loop(1, n_q, finish, pred[me_x * n_y + me_y])
    for v in range(vectors):
        out_ref[v] = total[v * group:(v + 1) * group]

    def drain(k, _):
        p_copy(k // n_y, lax.rem(k, n_y)).wait_send()
        return 0

    lax.fori_loop(1, n_q, drain, 0)
    for c in range(pairs):
        for hop in range(1, n_s):
            s_copy(hop, c).wait_send()
        grid.each(lambda d: h_copy(c, d).wait_send())
    grid.each(lambda d: e_copy(d).wait_send())


def per_device(sizes, records, kernel_block, diffusion):
    vectors, sensors, window = records.shape
    cells_x, cells_y = diffusion.shape
    points = cells_x * cells_y
    n_s, n_x, n_y = sizes
    n_q = n_x * n_y
    group = sensors // n_q
    half = window // 2
    pairs = vectors // 2
    steps = sensors // STEP
    halo = (cells_x + 2 * SWEEPS) * (cells_y + 2 * SWEEPS) - points
    tiles = (points + halo) // window
    around = len(DIRECTIONS)
    kernel_rows = kernel_block.reshape(sensors, points, window)
    rates = diffusion.T
    hops = max(n_s - 1, 1)
    dma = pltpu.SemaphoreType.DMA
    vmem = pltpu.VMEM
    return pl.pallas_call(
        functools.partial(kernel, sizes, vectors, sensors, cells_x, cells_y, window),
        out_shape=vmem((vectors, group, window), F32),
        in_specs=[pl.BlockSpec(memory_space=pl.ANY)] * 3,
        out_specs=pl.BlockSpec(memory_space=vmem),
        scratch_shapes=[
            vmem((vectors, sensors, window), BF16),
            vmem((vectors, sensors, window), F32),
            vmem((cells_y, cells_x), F32),
            vmem((cells_y, window), F32),
            vmem((around, cells_y, window), F32),
            vmem((cells_x + 2 * SWEEPS, 2 * cells_y, window), F32),
            vmem((sensors, points, window), BF16),
            vmem((3, sensors, points, window), BF16),
            vmem((2 * points, vectors * half), F32),
            vmem((pairs, 2, points, window), BF16),
            vmem((hops, pairs, 2, points, window), BF16),
            vmem((halo, points), BF16),
            vmem((pairs, 2, points, window), BF16),
            vmem((pairs, 2, points, window), BF16),
            vmem((pairs, 2, halo, window), BF16),
            vmem((pairs, 2, halo, window), BF16),
            vmem((tiles, points, window), BF16),
            vmem((tiles, points, window), BF16),
            vmem((4, vectors * half // 2, points), BF16),
            vmem((n_q, vectors * group, window), F32),
            vmem((max(n_q - 1, 1), vectors * group, window), F32),
            dma((2,)),
            dma((steps,)),
            *[dma((hops, pairs))] * 2,
            *[dma((around,))] * 2,
            *[dma((pairs, around))] * 2,
            *[dma((max(n_q - 1, 1),))] * 2,
            pltpu.SemaphoreType.REGULAR((max(max(n_x, n_y) - 3, 1),)),
        ],
        compiler_params=pltpu.CompilerParams(collective_id=0, has_side_effects=True),
    )(records, rates, kernel_rows)


def solution(mesh):
    sizes = tuple(mesh.shape[a] for a in ("sens", "sx", "sy"))
    return jax.shard_map(
        functools.partial(per_device, sizes),
        mesh=mesh,
        in_specs=(P(None, "sens", None), P("sens", "sx", "sy", None), P("sx", "sy")),
        out_specs=P(None, ("sens", "sx", "sy"), None),
        check_vma=False,
    )
```

```python
import functools

import jax
import jax.numpy as jnp
from jax import lax
from jax.experimental import pallas as pl
from jax.experimental.pallas import tpu as pltpu
from jax.sharding import PartitionSpec as P

SWEEPS = 4
MESH = pl.DeviceIdType.MESH
F32 = jnp.float32
BF16 = jnp.bfloat16
DIRECTIONS = ((-1, 0), (1, 0), (0, -1), (0, 1), (-1, -1), (-1, 1), (1, -1), (1, 1))
STEP = 16
PACK = 16
GROUP = 2
WIDE = 4
BATCHES = (2, 6)
NT = (((1,), (1,)), ((), ()))


def opposite(d):
    dx, dy = DIRECTIONS[d]
    return DIRECTIONS.index((-dx, -dy))


def iota(shape, axis):
    return lax.broadcasted_iota(jnp.int32, shape, axis)


class Grid:
    def __init__(self, sizes, cells_x, cells_y):
        self.nx, self.ny = sizes
        self.cx, self.cy, self.m = cells_x, cells_y, SWEEPS
        self.points = cells_x * cells_y
        self.counts = [self.m * self.cy if dy == 0 else self.cx * self.m if dx == 0 else self.m * self.m
                       for dx, dy in DIRECTIONS]
        self.offsets = [sum(self.counts[:d]) for d in range(len(DIRECTIONS))]
        self.halo = sum(self.counts)
        self.mx, self.my = lax.axis_index("sx"), lax.axis_index("sy")

    def exists(self, d):
        dx, dy = DIRECTIONS[d]
        ok = jnp.bool_(True)
        if dx:
            ok = ok & (self.mx + dx >= 0) & (self.mx + dx < self.nx)
        if dy:
            ok = ok & (self.my + dy >= 0) & (self.my + dy < self.ny)
        return ok

    def each(self, act):
        for d in range(len(DIRECTIONS)):
            @pl.when(self.exists(d))
            def _():
                act(d)

    def neighbour(self, d):
        dx, dy = DIRECTIONS[d]
        return {"sx": self.mx + dx, "sy": self.my + dy}

    def neighbours(self):
        wide_x = 1 + (self.mx > 0).astype(jnp.int32) + (self.mx < self.nx - 1).astype(jnp.int32)
        wide_y = 1 + (self.my > 0).astype(jnp.int32) + (self.my < self.ny - 1).astype(jnp.int32)
        return wide_x * wide_y - 1

    def selection(self):
        rows = []
        for (dx, dy), count in zip(DIRECTIONS, self.counts):
            r, p = iota((count, self.points), 0), iota((count, self.points), 1)
            x0 = self.cx - self.m if dx > 0 else 0
            if dy == 0:
                source = x0 * self.cy + r
            else:
                y0 = self.cy - self.m if dy > 0 else 0
                source = (x0 + r // self.m) * self.cy + y0 + r % self.m
            rows.append((p == source).astype(F32))
        return jnp.concatenate(rows, axis=0).astype(BF16)

    def place(self, wide_x):
        if wide_x < self.m:
            return -1, wide_x
        if wide_x < self.m + self.cx:
            return 0, wide_x - self.m
        return 1, wide_x - self.m - self.cx

    def index(self, wide_x):
        at, local = self.place(wide_x)
        sub = iota((self.cy, 128), 0)

        def base(dy):
            return self.points + self.offsets[DIRECTIONS.index((at, dy))]

        own = (local * self.cy if at == 0 else base(0) + local * self.cy) + sub
        right = base(1) + local * self.m + sub
        left = base(-1) + local * self.m + sub - self.m
        return own, jnp.where(sub < self.m, right, left)


def row_sums(terms):
    row = iota(terms[0].shape, 0)

    def merge(a, b, take, shift):
        return jnp.where(take, a, b) + pltpu.roll(jnp.where(take, b, a), 8 - shift, 0)

    sides = []
    for o in range(2):
        pair = [merge(terms[o + 2 * e], terms[o + 2 * e + 4], ((row - o - 2 * e) & 7) < 4, 4) for e in range(2)]
        sides.append(merge(pair[0], pair[1], ((row - o) & 3) < 2, 2))
    return merge(sides[0], sides[1], (row & 1) == 0, 1)


def kernel(sizes, vectors, sensors, cells_x, cells_y, window,
           records_hbm, rates_hbm, kernel_hbm, out_ref,
           rec, recf, rates, tile_d, got_d, wide_d, kbuf, kshift, acc,
           part, got, select, hi, lo, halo_out, halo_in, map_hi, map_lo, inside, smooth_t, pred, pred_got,
           i_sem, k_sem, s_send, s_recv, d_send, d_recv, h_send, h_recv, p_send, p_recv, ready):
    n_s, n_x, n_y = sizes
    points = cells_x * cells_y
    half = window // 2
    pairs = vectors // 2
    n_q = n_x * n_y
    group = sensors // n_q
    steps = sensors // STEP
    me_s, me_x, me_y = lax.axis_index("sens"), lax.axis_index("sx"), lax.axis_index("sy")
    grid = Grid((n_x, n_y), cells_x, cells_y)

    r_copy = pltpu.make_async_copy(records_hbm, rec, i_sem.at[0])
    d_copy = pltpu.make_async_copy(rates_hbm, rates, i_sem.at[1])

    def k_copy(i):
        return pltpu.make_async_copy(
            kernel_hbm.at[pl.ds(i * STEP, STEP)], kbuf.at[pl.ds(i * STEP, STEP)], k_sem.at[i])

    r_copy.start()
    d_copy.start()
    for i in range(steps):
        k_copy(i).start()

    barrier = pltpu.get_barrier_semaphore()
    got_d[...] = jnp.zeros_like(got_d)
    halo_in[...] = jnp.zeros_like(halo_in)
    for k in range(1, n_s):
        pl.semaphore_signal(barrier, inc=1, device_id={"sens": lax.rem(me_s + k, n_s)}, device_id_type=MESH)
    grid.each(lambda d: pl.semaphore_signal(barrier, inc=1, device_id=grid.neighbour(d), device_id_type=MESH))

    lanes, rows = iota((PACK, window), 1), iota((PACK, window), 0)
    keep = [(lanes < window - half + 1 + PACK * j + rows).astype(F32).astype(BF16) for j in range(half // PACK)]
    late = (iota((points, window), 1) >= half).astype(F32).astype(BF16)

    r_copy.wait()
    for v in range(vectors):
        recf[v] = rec[v].astype(F32)

    def hankel(v, block, s):
        line = jnp.broadcast_to(block[s:s + 1], (PACK, window))
        seed = pltpu.roll(line, window - half + 1, 1, stride=1, stride_axis=0).astype(BF16)
        return jnp.concatenate(
            [(seed if j == 0 else pltpu.roll(seed, PACK * j, 1)) * keep[j] for j in range(half // PACK)], axis=0)

    def lagged(s):
        block = kbuf[s]
        moved = pltpu.roll(block, half, 1) * late
        kshift[0, s] = moved
        return jnp.concatenate([block, moved], axis=0)

    acc[...] = jnp.zeros_like(acc)

    def adjoint(i, _):
        k_copy(i).wait()
        blocks = [recf[v, pl.ds(pl.multiple_of(i * STEP, STEP), STEP)] for v in range(vectors)]
        for g in range(0, STEP, GROUP):
            rhs = jnp.concatenate([
                jnp.concatenate([hankel(v, blocks[v], s) for v in range(vectors)], axis=0) for s in range(g, g + GROUP)], axis=1)
            lhs = jnp.concatenate([lagged(i * STEP + s) for s in range(g, g + GROUP)], axis=1)
            acc[...] += lax.dot_general(lhs, rhs, NT, preferred_element_type=F32)
        return 0

    lax.fori_loop(0, steps, adjoint, 0)

    def s_copy(hop, c):
        return pltpu.make_async_remote_copy(
            src_ref=part.at[c], dst_ref=got.at[hop - 1, c],
            send_sem=s_send.at[hop - 1, c], recv_sem=s_recv.at[hop - 1, c],
            device_id={"sens": lax.rem(me_s + hop, n_s)}, device_id_type=MESH)

    def e_copy(d):
        return pltpu.make_async_remote_copy(
            src_ref=tile_d, dst_ref=got_d.at[opposite(d)], send_sem=d_send.at[d], recv_sem=d_recv.at[opposite(d)],
            device_id=grid.neighbour(d), device_id_type=MESH)

    def h_copy(c, d):
        o = opposite(d)
        return pltpu.make_async_remote_copy(
            src_ref=halo_out.at[c, :, pl.ds(grid.offsets[d], grid.counts[d])],
            dst_ref=halo_in.at[c, :, pl.ds(grid.offsets[o], grid.counts[o])],
            send_sem=h_send.at[c, d], recv_sem=h_recv.at[c, o],
            device_id=grid.neighbour(d), device_id_type=MESH)

    d_copy.wait()
    tile_d[...] = jnp.zeros_like(tile_d)
    tile_d[:, :cells_x] = rates[...]
    for c in range(pairs):
        for h in range(2):
            part[c, h] = acc[pl.ds(h * points, points), pl.ds(c * window, window)].astype(BF16)

    pl.semaphore_wait(barrier, n_s - 1 + grid.neighbours())
    for c in range(pairs):
        for hop in range(1, n_s):
            s_copy(hop, c).start()
    grid.each(lambda d: e_copy(d).start())
    select[...] = grid.selection()

    quarter = half // 2
    later = [(iota((points, window), 1) >= by).astype(F32).astype(BF16) for by in (quarter, half + quarter)]

    def shifts(i, _):
        for u in range(4):
            block = kbuf[4 * i + u]
            for j, by in enumerate((quarter, half + quarter)):
                kshift[j + 1, 4 * i + u] = pltpu.roll(block, by, 1) * later[j]
        return 0

    lax.fori_loop(0, sensors // 4, shifts, 0)

    def gather(c, _):
        for hop in range(1, n_s):
            s_copy(hop, c).wait_recv()
        for h in range(2):
            total = acc[pl.ds(h * points, points), pl.ds(pl.multiple_of(c * window, window), window)]
            for hop in range(1, n_s):
                total = total + got[hop - 1, c, h].astype(F32)
            top = total.astype(BF16)
            hi[c, h] = top
            lo[c, h] = (total - top.astype(F32)).astype(BF16)
        beside = jnp.dot(select[...], jnp.concatenate([hi[c, 0], hi[c, 1]], axis=1), preferred_element_type=F32)
        for h in range(2):
            halo_out[c, h] = beside[:, h * window:(h + 1) * window].astype(BF16)
        grid.each(lambda d: h_copy(c, d).start())
        return 0

    lax.fori_loop(0, pairs, gather, 0)

    reach = max(n_x, n_y) - 1

    def call(r):
        grid.each(lambda d: pl.semaphore_signal(ready.at[r], inc=1, device_id=grid.neighbour(d), device_id_type=MESH))

    def answer(r):
        pl.semaphore_wait(ready.at[r], grid.neighbours())

    grid.each(lambda d: e_copy(opposite(d)).wait_recv())
    if reach > 2:
        call(0)

    sub = iota((cells_y, window), 0)
    m = grid.m
    wide_x = cells_x + 2 * m
    for x in range(wide_x):
        where_x, local = grid.place(x)
        column = local + (cells_x - m if where_x < 0 else 0)

        def rate(dy):
            d = (where_x, dy)
            block = tile_d[...] if d == (0, 0) else got_d[DIRECTIONS.index(d)]
            return jnp.broadcast_to(block[:, column:column + 1], (cells_y, window))

        wide_d[x, pl.ds(0, cells_y)] = rate(0)
        wide_d[x, pl.ds(cells_y, cells_y)] = jnp.where(sub < m, rate(1), rate(-1))

    def sweep_map(t, _):
        lane = iota((cells_y, window), 1) + t * window
        units = []
        for x in range(wide_x):
            own, beside = grid.index(x)
            units.append(jnp.concatenate([(lane == own).astype(F32), (lane == beside).astype(F32)], axis=0))
        now = jnp.stack(units, axis=0)
        for repeat in range(SWEEPS):
            interior = now[1:-1]
            beside = now[2:] + now[:-2] + pltpu.roll(interior, 2 * cells_y - 1, 1) + pltpu.roll(interior, 1, 1)
            rate = wide_d[pl.ds(repeat + 1, cells_x + 2 * (m - repeat - 1))]
            now = interior + rate * (beside - 4.0 * interior)
        done = now[:, :cells_y].reshape(points, window)
        top = done.astype(BF16)
        map_hi[t] = top
        map_lo[t] = (done - top.astype(F32)).astype(BF16)
        return 0

    tiles = (points + grid.halo) // window
    lax.fori_loop(0, tiles, sweep_map, 0)

    turn_r, turn_c = iota((window, window), 0), iota((window, window), 1)
    turn = ((turn_r // half == turn_c // half) & (turn_r % half + turn_c % half == half - 1)).astype(F32).astype(BF16)

    def inner(c, _):
        tall = jnp.concatenate([jnp.concatenate([hi[c, h], lo[c, h], hi[c, h]], axis=0) for h in range(2)], axis=1)
        part_own = jnp.concatenate([map_hi[0], map_hi[0], map_lo[0]], axis=1)
        inside[c] = jnp.dot(part_own, tall, preferred_element_type=F32)
        return 0

    def smooth(c, _):
        grid.each(lambda d: h_copy(c, opposite(d)).wait_recv())
        outer = jnp.concatenate([ref[t] for ref in (map_hi, map_lo) for t in range(1, tiles)], axis=1)
        beside = jnp.concatenate([jnp.concatenate([halo_in[c, h]] * 2, axis=0) for h in range(2)], axis=1)
        done = inside[c] + jnp.dot(outer, beside, preferred_element_type=F32)
        for h in range(2):
            turned = lax.dot_general(
                turn, done[:, h * window:(h + 1) * window].astype(BF16), NT, preferred_element_type=F32).astype(BF16)
            for v in range(2):
                for e in range(2):
                    smooth_t[2 * h + e, pl.ds(pl.multiple_of((2 * c + v) * quarter, quarter), quarter)] = turned[
                        v * half + e * quarter:v * half + (e + 1) * quarter]
        return 0

    lanes8, rows8 = iota((8, window), 1), iota((8, window), 0)

    me_q = me_x * n_y + me_y

    def p_copy(q, slot):
        return pltpu.make_async_remote_copy(
            src_ref=pred.at[q], dst_ref=pred_got.at[slot], send_sem=p_send.at[q], recv_sem=p_recv.at[slot],
            device_id={"sx": q // n_y, "sy": lax.rem(q, n_y)}, device_id_type=MESH)

    def diagonal(tile):
        terms = [tile[8 * j:8 * j + 8] for j in range(quarter // 8)]
        by = 8
        while len(terms) > 1:
            terms = [a + jnp.where(lanes8 >= by, pltpu.roll(b, by, 1), 0.0) for a, b in zip(terms[::2], terms[1::2])]
            by *= 2
        return jnp.where(lanes8 >= rows8, pltpu.roll(terms[0], 0, 1, stride=1, stride_axis=0), 0.0)

    lax.fori_loop(0, pairs, inner, 0)
    lax.fori_loop(0, pairs, smooth, 0)
    if reach > 2:
        answer(0)
        for r in range(1, reach - 2):
            call(r)
            answer(r)

    lhs = jnp.concatenate([smooth_t[h] for h in range(4)], axis=1)
    def forward(batch, first, t, _):
        for u in range(batch):
            q = first + batch * t + u
            runs = [None] * (vectors * group)
            for g in range(0, group, WIDE):
                some = range(g, min(g + WIDE, group))
                rhs = jnp.concatenate([
                    jnp.concatenate([buf[q * group + s] for s in some], axis=1)
                    for buf in (kbuf, kshift.at[1], kshift.at[0], kshift.at[2])], axis=0)
                res = jnp.dot(lhs, rhs, preferred_element_type=F32)
                for v in range(vectors):
                    for s in some:
                        runs[v * group + s] = diagonal(
                            res[v * quarter:(v + 1) * quarter, (s - g) * window:(s - g + 1) * window])
            count = len(runs)
            runs += [jnp.zeros_like(runs[0])] * (-count % 8)
            pred[q] = jnp.concatenate([row_sums(runs[j:j + 8]) for j in range(0, len(runs), 8)], axis=0)[:count]
        for u in range(batch):
            @pl.when(first + batch * t + u != me_q)
            def _():
                p_copy(first + batch * t + u, me_q).start()
        return 0

    for first, count, most in ((0, n_y, BATCHES[0]), (n_y, n_q - n_y, BATCHES[1])):
        if count:
            batch = max(u for u in range(1, most + 1) if count % u == 0)
            lax.fori_loop(0, count // batch, functools.partial(forward, batch, first), 0)
    pred_got[me_q] = pred[me_q]

    grid.each(lambda d: e_copy(d).wait_send())
    for c in range(pairs):
        for hop in range(1, n_s):
            s_copy(hop, c).wait_send()
        grid.each(lambda d: h_copy(c, d).wait_send())
    def finish(q, _):
        @pl.when(q != me_q)
        def _():
            p_copy(q, q).wait_send()
            p_copy(q, q).wait_recv()
        return 0

    lax.fori_loop(0, n_q, finish, 0)
    total = pred_got[0]
    for q in range(1, n_q):
        total = total + pred_got[q]
    for v in range(vectors):
        out_ref[v] = total[v * group:(v + 1) * group]


def per_device(sizes, records, kernel_block, diffusion):
    vectors, sensors, window = records.shape
    cells_x, cells_y = diffusion.shape
    points = cells_x * cells_y
    n_s, n_x, n_y = sizes
    n_q = n_x * n_y
    group = sensors // n_q
    half = window // 2
    pairs = vectors // 2
    steps = sensors // STEP
    halo = (cells_x + 2 * SWEEPS) * (cells_y + 2 * SWEEPS) - points
    tiles = (points + halo) // window
    around = len(DIRECTIONS)
    kernel_rows = kernel_block.reshape(sensors, points, window)
    rates = diffusion.T
    hops = max(n_s - 1, 1)
    dma = pltpu.SemaphoreType.DMA
    vmem = pltpu.VMEM
    return pl.pallas_call(
        functools.partial(kernel, sizes, vectors, sensors, cells_x, cells_y, window),
        out_shape=vmem((vectors, group, window), F32),
        in_specs=[pl.BlockSpec(memory_space=pl.ANY)] * 3,
        out_specs=pl.BlockSpec(memory_space=vmem),
        scratch_shapes=[
            vmem((vectors, sensors, window), BF16),
            vmem((vectors, sensors, window), F32),
            vmem((cells_y, cells_x), F32),
            vmem((cells_y, window), F32),
            vmem((around, cells_y, window), F32),
            vmem((cells_x + 2 * SWEEPS, 2 * cells_y, window), F32),
            vmem((sensors, points, window), BF16),
            vmem((3, sensors, points, window), BF16),
            vmem((2 * points, vectors * half), F32),
            vmem((pairs, 2, points, window), BF16),
            vmem((hops, pairs, 2, points, window), BF16),
            vmem((halo, points), BF16),
            vmem((pairs, 2, points, window), BF16),
            vmem((pairs, 2, points, window), BF16),
            vmem((pairs, 2, halo, window), BF16),
            vmem((pairs, 2, halo, window), BF16),
            vmem((tiles, points, window), BF16),
            vmem((tiles, points, window), BF16),
            vmem((pairs, points, 2 * window), F32),
            vmem((4, vectors * half // 2, points), BF16),
            vmem((n_q, vectors * group, window), F32),
            vmem((n_q, vectors * group, window), F32),
            dma((2,)),
            dma((steps,)),
            *[dma((hops, pairs))] * 2,
            *[dma((around,))] * 2,
            *[dma((pairs, around))] * 2,
            *[dma((n_q,))] * 2,
            pltpu.SemaphoreType.REGULAR((max(max(n_x, n_y) - 3, 1),)),
        ],
        compiler_params=pltpu.CompilerParams(collective_id=0, has_side_effects=True),
    )(records, rates, kernel_rows)


def solution(mesh):
    sizes = tuple(mesh.shape[a] for a in ("sens", "sx", "sy"))
    return jax.shard_map(
        functools.partial(per_device, sizes),
        mesh=mesh,
        in_specs=(P(None, "sens", None), P("sens", "sx", "sy", None), P("sx", "sy")),
        out_specs=P(None, ("sens", "sx", "sy"), None),
        check_vma=False,
    )
```

```python
import functools

import jax
import jax.numpy as jnp
from jax import lax
from jax.experimental import pallas as pl
from jax.experimental.pallas import tpu as pltpu
from jax.sharding import PartitionSpec as P

SWEEPS = 4
MESH = pl.DeviceIdType.MESH
F32 = jnp.float32
BF16 = jnp.bfloat16
DIRECTIONS = ((-1, -1), (-1, 1), (1, -1), (1, 1), (-1, 0), (1, 0), (0, -1), (0, 1))
STEP = 16
PACK = 16
GROUP = 2
WIDE = 4
BATCHES = (2, 12)
NT = (((1,), (1,)), ((), ()))


def opposite(d):
    dx, dy = DIRECTIONS[d]
    return DIRECTIONS.index((-dx, -dy))


def iota(shape, axis):
    return lax.broadcasted_iota(jnp.int32, shape, axis)


class Grid:
    def __init__(self, sizes, cells_x, cells_y):
        self.nx, self.ny = sizes
        self.cx, self.cy, self.m = cells_x, cells_y, SWEEPS
        self.points = cells_x * cells_y
        self.counts = [self.m * self.cy if dy == 0 else self.cx * self.m if dx == 0 else -(-self.m * (self.m - 1) // 2 // 8) * 8
                       for dx, dy in DIRECTIONS]
        self.offsets = [sum(self.counts[:d]) for d in range(len(DIRECTIONS))]
        self.halo = (cells_x + 2 * self.m) * (cells_y + 2 * self.m) - self.points
        self.mx, self.my = lax.axis_index("sx"), lax.axis_index("sy")

    def exists(self, d):
        dx, dy = DIRECTIONS[d]
        ok = jnp.bool_(True)
        if dx:
            ok = ok & (self.mx + dx >= 0) & (self.mx + dx < self.nx)
        if dy:
            ok = ok & (self.my + dy >= 0) & (self.my + dy < self.ny)
        return ok

    def each(self, act):
        for d in range(len(DIRECTIONS)):
            @pl.when(self.exists(d))
            def _():
                act(d)

    def neighbour(self, d):
        dx, dy = DIRECTIONS[d]
        return {"sx": self.mx + dx, "sy": self.my + dy}

    def neighbours(self):
        wide_x = 1 + (self.mx > 0).astype(jnp.int32) + (self.mx < self.nx - 1).astype(jnp.int32)
        wide_y = 1 + (self.my > 0).astype(jnp.int32) + (self.my < self.ny - 1).astype(jnp.int32)
        return wide_x * wide_y - 1

    def corner(self, d):
        far = [[self.m - i if step < 0 else i + 1 for i in range(self.m)] for step in DIRECTIONS[d]]
        return [(x, y) for x in range(self.m) for y in range(self.m) if far[0][x] + far[1][y] <= self.m]

    def selection(self):
        rows = []
        for d, ((dx, dy), count) in enumerate(zip(DIRECTIONS, self.counts)):
            r, p = iota((count, self.points), 0), iota((count, self.points), 1)
            x0 = self.cx - self.m if dx > 0 else 0
            if dy == 0:
                source = x0 * self.cy + r
            else:
                y0 = self.cy - self.m if dy > 0 else 0
                source = (x0 + r // self.m) * self.cy + y0 + r % self.m
                if dx:
                    source = jnp.full_like(r, -1)
                    for k, (x, y) in enumerate(self.corner(opposite(d))):
                        source = jnp.where(r == k, (x0 + x) * self.cy + y0 + y, source)
            rows.append((p == source).astype(F32))
        rows.append(jnp.zeros((self.halo - sum(self.counts), self.points), F32))
        return jnp.concatenate(rows, axis=0).astype(BF16)

    def place(self, wide_x):
        if wide_x < self.m:
            return -1, wide_x
        if wide_x < self.m + self.cx:
            return 0, wide_x - self.m
        return 1, wide_x - self.m - self.cx

    def index(self, wide_x):
        at, local = self.place(wide_x)
        sub = iota((self.cy, 128), 0)

        def base(dy):
            return self.points + self.offsets[DIRECTIONS.index((at, dy))]

        own = (local * self.cy if at == 0 else base(0) + local * self.cy) + sub
        if at:
            beside = jnp.full_like(sub, -1)
            for dy in (-1, 1):
                for k, (x, y) in enumerate(self.corner(DIRECTIONS.index((at, dy)))):
                    if x == local:
                        beside = jnp.where(sub == y + (self.m if dy < 0 else 0), base(dy) + k, beside)
            return own, beside
        right = base(1) + local * self.m + sub
        left = base(-1) + local * self.m + sub - self.m
        return own, jnp.where(sub < self.m, right, left)


def row_sums(terms):
    row = iota(terms[0].shape, 0)

    def merge(a, b, take, shift):
        return jnp.where(take, a, b) + pltpu.roll(jnp.where(take, b, a), 8 - shift, 0)

    sides = []
    for o in range(2):
        pair = [merge(terms[o + 2 * e], terms[o + 2 * e + 4], ((row - o - 2 * e) & 7) < 4, 4) for e in range(2)]
        sides.append(merge(pair[0], pair[1], ((row - o) & 3) < 2, 2))
    return merge(sides[0], sides[1], (row & 1) == 0, 1)


def kernel(sizes, vectors, sensors, cells_x, cells_y, window,
           records_hbm, rates_hbm, kernel_hbm, out_ref,
           rec, recf, rates, tile_d, got_d, wide_d, kbuf, kshift, acc,
           part, got, select, hi, lo, halo_out, halo_in, map_hi, map_lo, inside, smooth_t, pred, pred_got,
           i_sem, k_sem, s_send, s_recv, d_send, d_recv, h_send, h_recv, p_send, p_recv, ready):
    n_s, n_x, n_y = sizes
    points = cells_x * cells_y
    half = window // 2
    pairs = vectors // 2
    n_q = n_x * n_y
    group = sensors // n_q
    steps = sensors // STEP
    me_s, me_x, me_y = lax.axis_index("sens"), lax.axis_index("sx"), lax.axis_index("sy")
    grid = Grid((n_x, n_y), cells_x, cells_y)

    r_copy = pltpu.make_async_copy(records_hbm, rec, i_sem.at[0])
    d_copy = pltpu.make_async_copy(rates_hbm, rates, i_sem.at[1])

    def k_copy(i):
        return pltpu.make_async_copy(
            kernel_hbm.at[pl.ds(i * STEP, STEP)], kbuf.at[pl.ds(i * STEP, STEP)], k_sem.at[i])

    r_copy.start()
    d_copy.start()
    for i in range(steps):
        k_copy(i).start()

    barrier = pltpu.get_barrier_semaphore()
    got_d[...] = jnp.zeros_like(got_d)
    halo_in[...] = jnp.zeros_like(halo_in)
    for k in range(1, n_s):
        pl.semaphore_signal(barrier, inc=1, device_id={"sens": lax.rem(me_s + k, n_s)}, device_id_type=MESH)
    grid.each(lambda d: pl.semaphore_signal(barrier, inc=1, device_id=grid.neighbour(d), device_id_type=MESH))

    lanes, rows = iota((PACK, window), 1), iota((PACK, window), 0)
    keep = [(lanes < window - half + 1 + PACK * j + rows).astype(F32).astype(BF16) for j in range(half // PACK)]
    late = (iota((points, window), 1) >= half).astype(F32).astype(BF16)

    r_copy.wait()
    for v in range(vectors):
        recf[v] = rec[v].astype(F32)

    def hankel(v, block, s):
        line = jnp.broadcast_to(block[s:s + 1], (PACK, window))
        seed = pltpu.roll(line, window - half + 1, 1, stride=1, stride_axis=0).astype(BF16)
        return jnp.concatenate(
            [(seed if j == 0 else pltpu.roll(seed, PACK * j, 1)) * keep[j] for j in range(half // PACK)], axis=0)

    def lagged(s):
        block = kbuf[s]
        moved = pltpu.roll(block, half, 1) * late
        kshift[0, s] = moved
        return jnp.concatenate([block, moved], axis=0)

    acc[...] = jnp.zeros_like(acc)

    def adjoint(i, _):
        k_copy(i).wait()
        blocks = [recf[v, pl.ds(pl.multiple_of(i * STEP, STEP), STEP)] for v in range(vectors)]
        for g in range(0, STEP, GROUP):
            rhs = jnp.concatenate([
                jnp.concatenate([hankel(v, blocks[v], s) for v in range(vectors)], axis=0) for s in range(g, g + GROUP)], axis=1)
            lhs = jnp.concatenate([lagged(i * STEP + s) for s in range(g, g + GROUP)], axis=1)
            acc[...] += lax.dot_general(lhs, rhs, NT, preferred_element_type=F32)
        return 0

    lax.fori_loop(0, steps, adjoint, 0)

    def s_copy(hop, c):
        return pltpu.make_async_remote_copy(
            src_ref=part.at[c], dst_ref=got.at[hop - 1, c],
            send_sem=s_send.at[hop - 1, c], recv_sem=s_recv.at[hop - 1, c],
            device_id={"sens": lax.rem(me_s + hop, n_s)}, device_id_type=MESH)

    def e_copy(d):
        return pltpu.make_async_remote_copy(
            src_ref=tile_d, dst_ref=got_d.at[opposite(d)], send_sem=d_send.at[d], recv_sem=d_recv.at[opposite(d)],
            device_id=grid.neighbour(d), device_id_type=MESH)

    def h_copy(c, d):
        o = opposite(d)
        return pltpu.make_async_remote_copy(
            src_ref=halo_out.at[c, :, pl.ds(grid.offsets[d], grid.counts[d])],
            dst_ref=halo_in.at[c, :, pl.ds(grid.offsets[o], grid.counts[o])],
            send_sem=h_send.at[c, d], recv_sem=h_recv.at[c, o],
            device_id=grid.neighbour(d), device_id_type=MESH)

    d_copy.wait()
    tile_d[...] = jnp.zeros_like(tile_d)
    tile_d[:, :cells_x] = rates[...]
    for c in range(pairs):
        for h in range(2):
            part[c, h] = acc[pl.ds(h * points, points), pl.ds(c * window, window)].astype(BF16)

    pl.semaphore_wait(barrier, n_s - 1 + grid.neighbours())
    for c in range(pairs):
        for hop in range(1, n_s):
            s_copy(hop, c).start()
    grid.each(lambda d: e_copy(d).start())
    select[...] = grid.selection()

    quarter = half // 2
    later = [(iota((points, window), 1) >= by).astype(F32).astype(BF16) for by in (quarter, half + quarter)]

    def shifts(i, _):
        for u in range(4):
            block = kbuf[4 * i + u]
            for j, by in enumerate((quarter, half + quarter)):
                kshift[j + 1, 4 * i + u] = pltpu.roll(block, by, 1) * later[j]
        return 0

    lax.fori_loop(0, sensors // 4, shifts, 0)

    def gather(c, _):
        for hop in range(1, n_s):
            s_copy(hop, c).wait_recv()
        for h in range(2):
            total = acc[pl.ds(h * points, points), pl.ds(pl.multiple_of(c * window, window), window)]
            for hop in range(1, n_s):
                total = total + got[hop - 1, c, h].astype(F32)
            top = total.astype(BF16)
            hi[c, h] = top
            lo[c, h] = (total - top.astype(F32)).astype(BF16)
        beside = jnp.dot(select[...], jnp.concatenate([hi[c, 0], hi[c, 1]], axis=1), preferred_element_type=F32)
        for h in range(2):
            halo_out[c, h] = beside[:, h * window:(h + 1) * window].astype(BF16)
        grid.each(lambda d: h_copy(c, d).start())
        return 0

    lax.fori_loop(0, pairs, gather, 0)

    reach = max(n_x, n_y) - 1

    def call(r):
        grid.each(lambda d: pl.semaphore_signal(ready.at[r], inc=1, device_id=grid.neighbour(d), device_id_type=MESH))

    def answer(r):
        pl.semaphore_wait(ready.at[r], grid.neighbours())

    grid.each(lambda d: e_copy(opposite(d)).wait_recv())
    if reach > 2:
        call(0)

    sub = iota((cells_y, window), 0)
    m = grid.m
    wide_x = cells_x + 2 * m
    for x in range(wide_x):
        where_x, local = grid.place(x)
        column = local + (cells_x - m if where_x < 0 else 0)

        def rate(dy):
            d = (where_x, dy)
            block = tile_d[...] if d == (0, 0) else got_d[DIRECTIONS.index(d)]
            return jnp.broadcast_to(block[:, column:column + 1], (cells_y, window))

        wide_d[x, pl.ds(0, cells_y)] = rate(0)
        wide_d[x, pl.ds(cells_y, cells_y)] = jnp.where(sub < m, rate(1), rate(-1))

    def sweep_map(t, _):
        lane = iota((cells_y, window), 1) + t * window
        units = []
        for x in range(wide_x):
            own, beside = grid.index(x)
            units.append(jnp.concatenate([(lane == own).astype(F32), (lane == beside).astype(F32)], axis=0))
        now = jnp.stack(units, axis=0)
        for repeat in range(SWEEPS):
            interior = now[1:-1]
            beside = now[2:] + now[:-2] + pltpu.roll(interior, 2 * cells_y - 1, 1) + pltpu.roll(interior, 1, 1)
            rate = wide_d[pl.ds(repeat + 1, cells_x + 2 * (m - repeat - 1))]
            now = interior + rate * (beside - 4.0 * interior)
        done = now[:, :cells_y].reshape(points, window)
        top = done.astype(BF16)
        map_hi[t] = top
        map_lo[t] = (done - top.astype(F32)).astype(BF16)
        return 0

    tiles = (points + grid.halo) // window
    lax.fori_loop(0, tiles, sweep_map, 0)

    turn_r, turn_c = iota((window, window), 0), iota((window, window), 1)
    turn = ((turn_r // half == turn_c // half) & (turn_r % half + turn_c % half == half - 1)).astype(F32).astype(BF16)

    def inner(c, _):
        tall = jnp.concatenate([jnp.concatenate([hi[c, h], lo[c, h], hi[c, h]], axis=0) for h in range(2)], axis=1)
        part_own = jnp.concatenate([map_hi[0], map_hi[0], map_lo[0]], axis=1)
        inside[c] = jnp.dot(part_own, tall, preferred_element_type=F32)
        return 0

    def smooth(c, _):
        grid.each(lambda d: h_copy(c, opposite(d)).wait_recv())
        outer = jnp.concatenate([ref[t] for ref in (map_hi, map_lo) for t in range(1, tiles)], axis=1)
        beside = jnp.concatenate([jnp.concatenate([halo_in[c, h]] * 2, axis=0) for h in range(2)], axis=1)
        done = inside[c] + jnp.dot(outer, beside, preferred_element_type=F32)
        for h in range(2):
            turned = lax.dot_general(
                turn, done[:, h * window:(h + 1) * window].astype(BF16), NT, preferred_element_type=F32).astype(BF16)
            for v in range(2):
                for e in range(2):
                    smooth_t[2 * h + e, pl.ds(pl.multiple_of((2 * c + v) * quarter, quarter), quarter)] = turned[
                        v * half + e * quarter:v * half + (e + 1) * quarter]
        return 0

    lanes8, rows8 = iota((8, window), 1), iota((8, window), 0)

    me_q = me_x * n_y + me_y

    def p_copy(q, slot):
        return pltpu.make_async_remote_copy(
            src_ref=pred.at[q], dst_ref=pred_got.at[slot], send_sem=p_send.at[q], recv_sem=p_recv.at[slot],
            device_id={"sx": q // n_y, "sy": lax.rem(q, n_y)}, device_id_type=MESH)

    def diagonal(tile):
        terms = [tile[8 * j:8 * j + 8] for j in range(quarter // 8)]
        by = 8
        while len(terms) > 1:
            terms = [a + jnp.where(lanes8 >= by, pltpu.roll(b, by, 1), 0.0) for a, b in zip(terms[::2], terms[1::2])]
            by *= 2
        return jnp.where(lanes8 >= rows8, pltpu.roll(terms[0], 0, 1, stride=1, stride_axis=0), 0.0)

    lax.fori_loop(0, pairs, inner, 0)
    lax.fori_loop(0, pairs, smooth, 0)
    if reach > 2:
        answer(0)
        for r in range(1, reach - 2):
            call(r)
            answer(r)

    lhs = jnp.concatenate([smooth_t[h] for h in range(4)], axis=1)
    def forward(batch, first, t, _):
        for u in range(batch):
            q = first + batch * t + u
            runs = [None] * (vectors * group)
            for g in range(0, group, WIDE):
                some = range(g, min(g + WIDE, group))
                rhs = jnp.concatenate([
                    jnp.concatenate([buf[q * group + s] for s in some], axis=1)
                    for buf in (kbuf, kshift.at[1], kshift.at[0], kshift.at[2])], axis=0)
                res = jnp.dot(lhs, rhs, preferred_element_type=F32)
                for v in range(vectors):
                    for s in some:
                        runs[v * group + s] = diagonal(
                            res[v * quarter:(v + 1) * quarter, (s - g) * window:(s - g + 1) * window])
            count = len(runs)
            runs += [jnp.zeros_like(runs[0])] * (-count % 8)
            pred[q] = jnp.concatenate([row_sums(runs[j:j + 8]) for j in range(0, len(runs), 8)], axis=0)[:count]
        for u in range(batch):
            @pl.when(first + batch * t + u != me_q)
            def _():
                p_copy(first + batch * t + u, me_q).start()
        return 0

    for first, count, most in ((0, n_y, BATCHES[0]), (n_y, n_q - n_y, BATCHES[1])):
        if count:
            batch = max(u for u in range(1, most + 1) if count % u == 0)
            lax.fori_loop(0, count // batch, functools.partial(forward, batch, first), 0)
    pred_got[me_q] = pred[me_q]

    grid.each(lambda d: e_copy(d).wait_send())
    for c in range(pairs):
        for hop in range(1, n_s):
            s_copy(hop, c).wait_send()
        grid.each(lambda d: h_copy(c, d).wait_send())
    def finish(q, _):
        @pl.when(q != me_q)
        def _():
            p_copy(q, q).wait_send()
            p_copy(q, q).wait_recv()
        return 0

    lax.fori_loop(0, n_q, finish, 0)
    total = pred_got[0]
    for q in range(1, n_q):
        total = total + pred_got[q]
    for v in range(vectors):
        out_ref[v] = total[v * group:(v + 1) * group]


def per_device(sizes, records, kernel_block, diffusion):
    vectors, sensors, window = records.shape
    cells_x, cells_y = diffusion.shape
    points = cells_x * cells_y
    n_s, n_x, n_y = sizes
    n_q = n_x * n_y
    group = sensors // n_q
    half = window // 2
    pairs = vectors // 2
    steps = sensors // STEP
    halo = (cells_x + 2 * SWEEPS) * (cells_y + 2 * SWEEPS) - points
    tiles = (points + halo) // window
    around = len(DIRECTIONS)
    kernel_rows = kernel_block.reshape(sensors, points, window)
    rates = diffusion.T
    hops = max(n_s - 1, 1)
    dma = pltpu.SemaphoreType.DMA
    vmem = pltpu.VMEM
    return pl.pallas_call(
        functools.partial(kernel, sizes, vectors, sensors, cells_x, cells_y, window),
        out_shape=vmem((vectors, group, window), F32),
        in_specs=[pl.BlockSpec(memory_space=pl.ANY)] * 3,
        out_specs=pl.BlockSpec(memory_space=vmem),
        scratch_shapes=[
            vmem((vectors, sensors, window), BF16),
            vmem((vectors, sensors, window), F32),
            vmem((cells_y, cells_x), F32),
            vmem((cells_y, window), F32),
            vmem((around, cells_y, window), F32),
            vmem((cells_x + 2 * SWEEPS, 2 * cells_y, window), F32),
            vmem((sensors, points, window), BF16),
            vmem((3, sensors, points, window), BF16),
            vmem((2 * points, vectors * half), F32),
            vmem((pairs, 2, points, window), BF16),
            vmem((hops, pairs, 2, points, window), BF16),
            vmem((halo, points), BF16),
            vmem((pairs, 2, points, window), BF16),
            vmem((pairs, 2, points, window), BF16),
            vmem((pairs, 2, halo, window), BF16),
            vmem((pairs, 2, halo, window), BF16),
            vmem((tiles, points, window), BF16),
            vmem((tiles, points, window), BF16),
            vmem((pairs, points, 2 * window), F32),
            vmem((4, vectors * half // 2, points), BF16),
            vmem((n_q, vectors * group, window), F32),
            vmem((n_q, vectors * group, window), F32),
            dma((2,)),
            dma((steps,)),
            *[dma((hops, pairs))] * 2,
            *[dma((around,))] * 2,
            *[dma((pairs, around))] * 2,
            *[dma((n_q,))] * 2,
            pltpu.SemaphoreType.REGULAR((max(max(n_x, n_y) - 3, 1),)),
        ],
        compiler_params=pltpu.CompilerParams(collective_id=0, has_side_effects=True),
    )(records, rates, kernel_rows)


def solution(mesh):
    sizes = tuple(mesh.shape[a] for a in ("sens", "sx", "sy"))
    return jax.shard_map(
        functools.partial(per_device, sizes),
        mesh=mesh,
        in_specs=(P(None, "sens", None), P("sens", "sx", "sy", None), P("sx", "sy")),
        out_specs=P(None, ("sens", "sx", "sy"), None),
        check_vma=False,
    )
```
